256 devices in a mesh: wall: 16 (over x, z_lo), spec: 16 (over y, z_hi, core).
Axes of the slice: x: 4, y: 4, z: 8 (z_hi: 2, z_lo: 4; z = z_hi * 4 + z_lo), core: 2. Of those that a mesh axis runs over, the one named last changes fastest.
Arguments:
- signal: bfloat16 [4, 2, 512, 32, 10240], P(None, None, 'wall', None, 'spec'), may hold values from -6 to 6
- kx_index: int32 [128], replicated, may hold values from 0 to 5119
- kz_index: int32 [128], replicated, may hold values from 0 to 3
Outputs:
- phi: float32 [2, 128, 512, 512], P(None, 'spec', 'wall')
The draws below stay inside these ranges and needn't reach their ends.
Inputs may be any that keep to these rules, and one draw needn't show every extreme that they name: `kx_index`: pairs may repeat.
All inputs are finite; a program needn't handle non-finite values.
Results may differ from the reference program's by a relative error of at most 0.0042.
Values sent between devices are 32-bit elements; how exact they have to be, the bound alone decides.
No kernel may reach another device: no remote copies, remote signals or barrier semaphores. Data moves between devices by JAX's collectives and lax.ppermute only.
A program may use at most 64 MiB of HBM per device.

```python
import math
import jax
import jax.numpy as jnp
from jax import lax

NXW = 10240
K = 128
KZ = 4
SNAP = 32
NY = 512


def plant(result, rng, smallest, top_value):
    extent = result.shape
    index_at = [jax.random.randint(jax.random.fold_in(rng, axis), (), 0, extent[axis]) for axis in range(len(extent))]
    result = result.at[tuple(index_at)].set(smallest)
    longest = extent.index(max(extent))
    index_at[longest] = (index_at[longest] + 1) % extent[longest]
    return result.at[tuple(index_at)].set(top_value)


def steps_of(rng, shape, shards, least, high):
    loudness, own = 1.0, jax.random.fold_in(rng, 6)
    for axis_at, blocks in shards:
        draws = jnp.exp(jax.random.uniform(jax.random.fold_in(own, axis_at), (blocks,), jnp.float32, least / len(shards), high / len(shards)))
        loudness = loudness * jnp.repeat(draws, shape[axis_at] // blocks).reshape([-1 if axis == axis_at else 1 for axis in range(len(shape))])
    return loudness


def scatter_about(key, extent, spread, limit, split=(), held_as=jnp.bfloat16):
    array = jax.random.normal(key, extent, jnp.float32) * spread
    if len(split) > 0:
        array = steps_of(key, extent, split, -0.22, 0.18) * array
    return jnp.clip(array, min=-limit, max=limit).astype(held_as)


def setup_inputs(seed: int = 0) -> dict:
    arg_keys = jax.random.split(jax.random.key(seed), 4)
    signal = scatter_about(arg_keys[0], (KZ, 2, NY, SNAP, NXW), 1.0, 6.0, ((2, 16), (4, 16)))
    kx_index = plant(jax.random.randint(arg_keys[1], (K,), 0, NXW // 2), jax.random.fold_in(arg_keys[1], 1), 0, (NXW // 2) - 1).astype(jnp.int32)
    kz_index = plant(jax.random.randint(arg_keys[2], (K,), 0, KZ), jax.random.fold_in(arg_keys[2], 1), 0, KZ - 1).astype(jnp.int32)
    return dict(signal=signal, kx_index=kx_index, kz_index=kz_index)


def tables(kx_values, positions):
    phase = (kx_values[:, None] * positions[None, :]) % NXW
    angle = (2.0 * math.pi / NXW) * phase.astype(jnp.float32)
    factor = float(NXW) ** -0.5
    return (jnp.cos(angle) * factor).astype(jnp.bfloat16), (jnp.sin(angle) * factor).astype(jnp.bfloat16)


def reference(signal, kx_index, kz_index):
    modes, parts, planes, snaps, points = signal.shape
    flat = signal.reshape(modes, parts * planes * snaps, points)
    cosine, sine = tables(kx_index, jnp.arange(points, dtype=jnp.int32))

    def single(item):
        cos_row, sin_row, mode = item
        chosen = lax.dynamic_index_in_dim(flat, mode, 0, keepdims=False)
        basis = jnp.stack([cos_row, sin_row], 1)
        product = jnp.dot(chosen, basis, preferred_element_type=jnp.float32).reshape(2, planes * snaps, 2)
        real = product[0, :, 0] + product[1, :, 1]
        imag = product[1, :, 0] - product[0, :, 1]
        return jnp.stack([real, imag])

    spectra = lax.map(single, (cosine, sine, kz_index)).reshape(-1, 2, planes, snaps)
    first = spectra[:, 0]
    second = spectra[:, 1]
    high = lax.Precision.HIGHEST
    real = (jnp.einsum('kys,kzs->kyz', first, first, precision=high) + jnp.einsum('kys,kzs->kyz', second, second, precision=high)) / SNAP
    imag = (jnp.einsum('kys,kzs->kyz', second, first, precision=high) - jnp.einsum('kys,kzs->kyz', first, second, precision=high)) / SNAP
    return jnp.stack([real, imag])
```

```python
import math

import jax
import jax.numpy as jnp
from jax import lax
from jax.experimental import pallas as pl
from jax.experimental.pallas import tpu as pltpu
from jax.sharding import Mesh
from jax.sharding import PartitionSpec as P

NXW = 10240
QUARTER = NXW // 4
SIN = (1.0, -1.0 / 6, 1.0 / 120, -1.0 / 5040, 1.0 / 362880)
COS = (1.0, -0.5, 1.0 / 24, -1.0 / 720, 1.0 / 40320)
FINE = ("x", "zl", "y", "zh", "core")
WALL, SPEC = FINE[:2], FINE[2:]
VMEM = pl.BlockSpec(memory_space=pltpu.VMEM)
SMEM = pl.BlockSpec(memory_space=pltpu.SMEM)
HBM = pl.BlockSpec(memory_space=pl.ANY)
PARAMS = pltpu.CompilerParams(vmem_limit_bytes=48 * 2**20)


def horner(coefficients, square):
    total = jnp.full_like(square, coefficients[-1])
    for value in coefficients[-2::-1]:
        total = total * square + value
    return total


def basis_columns(kx_row, positions):
    product = positions * kx_row
    quarter = jnp.floor(product.astype(jnp.float32) * (1.0 / QUARTER) + 0.5).astype(jnp.int32)
    angle = (product - quarter * QUARTER).astype(jnp.float32) * (2.0 * math.pi / NXW)
    square = angle * angle
    sine = horner(SIN, square) * angle
    cosine = horner(COS, square)
    swap = (quarter & 1) == 1
    factor = float(NXW) ** -0.5
    first = jnp.where(swap, sine, cosine) * factor
    second = jnp.where(swap, cosine, sine) * factor
    first = jnp.where(((quarter + 1) & 2) == 2, -first, first)
    second = jnp.where((quarter & 2) == 2, -second, second)
    return first.astype(jnp.bfloat16), second.astype(jnp.bfloat16)


def dft_kernel(place, kx_ref, kz_ref, signal, mine, other, held, basis, sems):
    modes, parts, quads, groups, snaps, width = signal.shape
    chunks = sems.shape[0]
    per = groups // chunks
    copies = []
    for t in range(chunks):
        part = pl.ds(t * per, per)
        copy = pltpu.make_async_copy(signal.at[:, :, :, part], held.at[:, :, :, part], sems.at[t])
        copy.start()
        copies.append(copy)
    pairs = kx_ref.shape[1]
    rows = lax.broadcasted_iota(jnp.int32, (width, pairs), 0) + place[0]
    cosine, sine = basis_columns(kx_ref[...], rows)
    basis[:width, :pairs] = cosine
    basis[:width, pairs:] = -sine
    basis[width:, :pairs] = sine
    basis[width:, pairs:] = cosine
    table = basis[...]
    kz = kz_ref[...]
    y, zh, core = place[1], place[2], place[3]
    for t in range(chunks):
        copies[t].wait()
        total = None
        for j in range(modes):
            lines = []
            for g in range(t * per, t * per + per):
                halves = [held[j, c, :, g].reshape(quads * snaps, width) for c in range(parts)]
                lines.append(jnp.concatenate(halves, axis=1))
            lines = jnp.concatenate(lines, axis=0)
            product = jnp.dot(lines, table, preferred_element_type=jnp.float32)
            if total is None:
                total = product
            else:
                total = jnp.where(jnp.concatenate([kz, kz], axis=1) == j, product, total)
        for i in range(per):
            g = t * per + i
            turned = total[i * 128 : (i + 1) * 128].T
            for yy in range(4):
                slot = (yy + 4 - y) & 3
                for zz in range(2):
                    for c in range(parts):
                        at = c * pairs + (yy * 4 + zz * 2) * 8
                        low, high = turned[at : at + 8], turned[at + 8 : at + 16]
                        mine[slot, zz ^ zh, c, g] = jnp.where(core == 0, low, high)
                        other[slot, zz ^ zh, c, g] = jnp.where(core == 0, high, low)


def dft(place, kx_index, kz_index, signal):
    modes, parts, planes, snaps, width = signal.shape
    pairs = kx_index.shape[0]
    view = signal.reshape(modes, parts, 4, planes // 4, snaps, width)
    chunks = 4
    block = jax.ShapeDtypeStruct((4, 2, parts, planes // 4, 8, 128), jnp.float32)
    return pl.pallas_call(
        dft_kernel,
        out_shape=(block, block),
        in_specs=[SMEM, VMEM, VMEM, HBM],
        out_specs=(VMEM, VMEM),
        scratch_shapes=[
            pltpu.VMEM(view.shape, signal.dtype),
            pltpu.VMEM((parts * width, 2 * pairs), jnp.bfloat16),
            pltpu.SemaphoreType.DMA((chunks,)),
        ],
        compiler_params=PARAMS,
        name="dft",
    )(place, kx_index.reshape(1, pairs), kz_index.reshape(1, pairs), view)


def turn_kernel(own_ref, came_ref, out_ref, total):
    total[...] = own_ref[...].reshape(total.shape) + came_ref[...].reshape(total.shape)
    lane = lax.broadcasted_iota(jnp.int32, (8, 128), 1) // 32
    for kk in range(4):
        tiles = []
        for k2 in range(2):
            for c in range(2):
                tiles.append(total[c, pl.ds(2 * kk + k2, 8, stride=8), :])
        for q in range(4):
            row = None
            for j, tile in enumerate(tiles):
                shift = ((j - q) * 32) % 128
                moved = tile if shift == 0 else pltpu.roll(tile, shift, 1)
                row = moved if row is None else jnp.where(lane == j, moved, row)
            out_ref[kk, q * 8 : (q + 1) * 8, :] = row


def turn(own, came):
    return pl.pallas_call(
        turn_kernel,
        out_shape=jax.ShapeDtypeStruct((4, 32, 128), jnp.float32),
        in_specs=[VMEM, VMEM],
        out_specs=VMEM,
        scratch_shapes=[pltpu.VMEM((2, 64, 128), jnp.float32)],
        compiler_params=PARAMS,
        name="turn",
    )(own, came)


def gram_kernel(place, own_ref, *refs):
    blocks, out_ref = refs[:-1], refs[-1]
    x = place[4]
    lane = lax.broadcasted_iota(jnp.int32, (32, 128), 1) // 32
    for kk in range(4):
        own = own_ref[kk] * (1.0 / 32)
        turned = jnp.where(lane % 2 == 0, pltpu.roll(own, 96, 1), -pltpu.roll(own, 32, 1))
        left = []
        for k2 in range(2):
            keep = lane // 2 == k2
            left.append(jnp.where(keep, own, 0.0))
            left.append(jnp.where(keep, turned, 0.0))
        left = jnp.concatenate(left, axis=0).astype(jnp.bfloat16)
        for i, block in enumerate(blocks):
            right = block[:, kk].reshape(128, 128).astype(jnp.bfloat16)
            product = lax.dot_general(
                left, right, (((1,), (1,)), ((), ())), preferred_element_type=jnp.float32
            )
            at = pl.multiple_of(((x + 4 - i) & 3) * 128, 128)
            for k2 in range(2):
                for c in range(2):
                    base = (k2 * 2 + c) * 32
                    out_ref[c, 2 * kk + k2, :, pl.ds(at, 128)] = product[base : base + 32]


def gram(place, own, blocks):
    return pl.pallas_call(
        gram_kernel,
        out_shape=jax.ShapeDtypeStruct((2, 8, 32, 512), jnp.float32),
        in_specs=[SMEM, VMEM] + [VMEM] * len(blocks),
        out_specs=VMEM,
        compiler_params=PARAMS,
        name="gram",
    )(place, own, *blocks)


def shifted(array, axis, by):
    size = lax.axis_size(axis)
    return lax.ppermute(array, axis, [(s, (s + by) % size) for s in range(size)])


def on_device(signal, kx_index, kz_index):
    width = signal.shape[-1]
    y, zh, core = (lax.axis_index(name) for name in SPEC)
    at = lax.axis_index(SPEC) * width
    place = jnp.stack([at, y, zh, core, lax.axis_index("x")]).astype(jnp.int32)
    mine, other = dft(place, kx_index, kz_index, signal)
    summed = mine + shifted(other, "core", 1)
    came = [shifted(summed[i], "y", i) for i in (1, 2, 3)]
    halves = summed[0] + came[0] + came[1] + came[2]
    own = turn(halves[0], shifted(halves[1], "zh", 1))
    column = lax.all_to_all(jnp.broadcast_to(own, (4, *own.shape)), "zl", 0, 0, tiled=True)
    blocks = [column] + [shifted(column, "x", i) for i in (1, 2, 3)]
    return gram(place, own, blocks)


def solution(mesh):
    fine = Mesh(mesh.devices.reshape(4, 4, 4, 2, 2), FINE)
    return jax.shard_map(
        on_device,
        mesh=fine,
        in_specs=(P(None, None, WALL, None, SPEC), P(), P()),
        out_specs=P(None, SPEC, WALL, None),
        check_vma=False,
    )
```

```python
import functools
import math

import jax
import jax.numpy as jnp
from jax import lax
from jax.experimental import pallas as pl
from jax.experimental.pallas import tpu as pltpu
from jax.sharding import Mesh
from jax.sharding import PartitionSpec as P

NXW = 10240
QUARTER = NXW // 4
SIN = (1.0, -1.0 / 6, 1.0 / 120, -1.0 / 5040, 1.0 / 362880)
COS = (1.0, -0.5, 1.0 / 24, -1.0 / 720, 1.0 / 40320)
FINE = ("x", "zl", "y", "zh", "core")
WALL, SPEC = FINE[:2], FINE[2:]
VMEM = pl.BlockSpec(memory_space=pltpu.VMEM)
SMEM = pl.BlockSpec(memory_space=pltpu.SMEM)
HBM = pl.BlockSpec(memory_space=pl.ANY)
FAR = pl.BlockSpec(memory_space=pltpu.HBM)
PARAMS = pltpu.CompilerParams(vmem_limit_bytes=48 * 2**20)


def horner(coefficients, square):
    total = jnp.full_like(square, coefficients[-1])
    for value in coefficients[-2::-1]:
        total = total * square + value
    return total


def basis_columns(kx_row, positions):
    product = positions * kx_row
    quarter = jnp.floor(product.astype(jnp.float32) * (1.0 / QUARTER) + 0.5).astype(jnp.int32)
    angle = (product - quarter * QUARTER).astype(jnp.float32) * (2.0 * math.pi / NXW)
    square = angle * angle
    sine = horner(SIN, square) * angle
    cosine = horner(COS, square)
    swap = (quarter & 1) == 1
    factor = float(NXW) ** -0.5
    first = jnp.where(swap, sine, cosine) * factor
    second = jnp.where(swap, cosine, sine) * factor
    first = jnp.where(((quarter + 1) & 2) == 2, -first, first)
    second = jnp.where((quarter & 2) == 2, -second, second)
    return first.astype(jnp.bfloat16), second.astype(jnp.bfloat16)


CHUNKS = (2, 2, 2, 2)


def dft_kernel(place, kx_hbm, kz_hbm, signal, mine, other, held, basis, kx_ref, kz_ref, sems):
    modes, parts, quads, groups, snaps, width = signal.shape
    pairs = kx_ref.shape[1]
    index = [
        pltpu.make_async_copy(kx_hbm, kx_ref, sems.at[len(CHUNKS)]),
        pltpu.make_async_copy(kz_hbm, kz_ref, sems.at[len(CHUNKS) + 1]),
    ]
    for copy in index:
        copy.start()
    copies, first = [], 0
    for t, size in enumerate(CHUNKS):
        part = pl.ds(first, size)
        copies.append(pltpu.make_async_copy(signal.at[:, :, :, part], held.at[:, :, :, part], sems.at[t]))
        copies[t].start()
        first += size
    for copy in index:
        copy.wait()
    rows = lax.broadcasted_iota(jnp.int32, (width, pairs), 0) + place[0]
    cosine, sine = basis_columns(kx_ref[...], rows)
    basis[:width, :pairs] = cosine
    basis[:width, pairs:] = -sine
    basis[width:, :pairs] = sine
    basis[width:, pairs:] = cosine
    kz = jnp.concatenate([kz_ref[...], kz_ref[...]], axis=1)
    y, zh, core = place[1], place[2], place[3]
    first = 0
    for t, size in enumerate(CHUNKS):
        copies[t].wait()
        total = None
        for j in range(modes):
            lines = []
            for g in range(first, first + size):
                halves = [held[j, c, :, g].reshape(quads * snaps, width) for c in range(parts)]
                lines.append(jnp.concatenate(halves, axis=1))
            lines = jnp.concatenate(lines, axis=0)
            product = jnp.dot(lines, basis[...], preferred_element_type=jnp.float32)
            total = product if total is None else jnp.where(kz == j, product, total)
        for i in range(size):
            turned = total[i * 128 : (i + 1) * 128].T
            for yy in range(4):
                slot = (yy + 4 - y) & 3
                for zz in range(2):
                    for c in range(parts):
                        at = c * pairs + (yy * 4 + zz * 2) * 8
                        low, high = turned[at : at + 8], turned[at + 8 : at + 16]
                        mine[slot, zz ^ zh, c, first + i] = jnp.where(core == 0, low, high)
                        other[slot, zz ^ zh, c, first + i] = jnp.where(core == 0, high, low)
        first += size


def dft(place, kx_index, kz_index, signal):
    modes, parts, planes, snaps, width = signal.shape
    pairs = kx_index.shape[0]
    view = signal.reshape(modes, parts, 4, planes // 4, snaps, width)
    block = jax.ShapeDtypeStruct((4, 2, parts, planes // 4, 8, 128), jnp.float32)
    return pl.pallas_call(
        dft_kernel,
        out_shape=(block, block),
        in_specs=[SMEM, FAR, FAR, HBM],
        out_specs=(VMEM, VMEM),
        scratch_shapes=[
            pltpu.VMEM(view.shape, signal.dtype),
            pltpu.VMEM((parts * width, 2 * pairs), jnp.bfloat16),
            pltpu.VMEM((1, pairs), jnp.int32),
            pltpu.VMEM((1, pairs), jnp.int32),
            pltpu.SemaphoreType.DMA((len(CHUNKS) + 2,)),
        ],
        compiler_params=PARAMS,
        name="dft",
    )(
        place,
        pltpu.with_memory_space_constraint(kx_index.reshape(1, pairs), pltpu.HBM),
        pltpu.with_memory_space_constraint(kz_index.reshape(1, pairs), pltpu.HBM),
        view,
    )


def turn_kernel(own_ref, came_ref, out_ref, total):
    total[...] = own_ref[...].reshape(total.shape) + came_ref[...].reshape(total.shape)
    lane = lax.broadcasted_iota(jnp.int32, (8, 128), 1) // 32
    for kk in range(4):
        tiles = []
        for k2 in range(2):
            for c in range(2):
                tiles.append(total[c, pl.ds(2 * kk + k2, 8, stride=8), :])
        for q in range(4):
            row = None
            for j, tile in enumerate(tiles):
                shift = ((j - q) * 32) % 128
                moved = tile if shift == 0 else pltpu.roll(tile, shift, 1)
                row = moved if row is None else jnp.where(lane == j, moved, row)
            out_ref[kk, q * 8 : (q + 1) * 8, :] = row


def turn(own, came):
    return pl.pallas_call(
        turn_kernel,
        out_shape=jax.ShapeDtypeStruct((4, 32, 128), jnp.float32),
        in_specs=[VMEM, VMEM],
        out_specs=VMEM,
        scratch_shapes=[pltpu.VMEM((2, 64, 128), jnp.float32)],
        compiler_params=PARAMS,
        name="turn",
    )(own, came)


def against(left, right):
    return lax.dot_general(left, right, (((1,), (1,)), ((), ())), preferred_element_type=jnp.float32)


def gram_kernel(spots, place, own_ref, *refs):
    blocks, (out_hbm, right, out, sems) = refs[:-4], refs[-4:]
    x, zl = place[4], place[5]
    lane = lax.broadcasted_iota(jnp.int32, (32, 128), 1) // 32
    copies = []
    for kk in range(4):
        for block, group in zip(blocks, spots):
            for n, (i, j) in enumerate(group):
                at = pl.multiple_of(((x ^ i) * 4 + (zl ^ j)) * 32, 32)
                right[kk, pl.ds(at, 32), :] = block[n, kk].astype(jnp.bfloat16)
        own = own_ref[kk] * (1.0 / 32)
        turned = jnp.where(lane % 2 == 0, pltpu.roll(own, 96, 1), -pltpu.roll(own, 32, 1))
        left = []
        for k2 in range(2):
            keep = lane // 2 == k2
            left.append(jnp.where(keep, own, 0.0))
            left.append(jnp.where(keep, turned, 0.0))
        whole = jnp.concatenate(left, axis=0)
        high = whole.astype(jnp.bfloat16)
        low = (whole - high.astype(jnp.float32)).astype(jnp.bfloat16)
        product = against(jnp.concatenate([high, low], axis=1), jnp.concatenate([right[kk], right[kk]], axis=1))
        for k2 in range(2):
            for c in range(2):
                base = (k2 * 2 + c) * 32
                out[c, 2 * kk + k2] = product[base : base + 32]
        part = pl.ds(2 * kk, 2)
        copies.append(pltpu.make_async_copy(out.at[:, part], out_hbm.at[:, part], sems.at[kk]))
        copies[kk].start()
    for copy in copies:
        copy.wait()


def gram(place, own, blocks, spots):
    shape = (2, 8, 32, 512)
    return pl.pallas_call(
        functools.partial(gram_kernel, spots),
        out_shape=jax.ShapeDtypeStruct(shape, jnp.float32),
        in_specs=[SMEM, VMEM] + [VMEM] * len(blocks),
        out_specs=HBM,
        scratch_shapes=[
            pltpu.VMEM((4, 512, 128), jnp.bfloat16),
            pltpu.VMEM(shape, jnp.float32),
            pltpu.SemaphoreType.DMA((4,)),
        ],
        compiler_params=PARAMS,
        name="gram",
    )(place, own, *blocks)


def shifted(array, axis, by):
    size = lax.axis_size(axis)
    return lax.ppermute(array, axis, [(s, (s + by) % size) for s in range(size)])


def swapped(array, axis, by):
    return lax.ppermute(array, axis, [(s, s ^ by) for s in range(lax.axis_size(axis))])


def gathered(own):
    z3, z2 = (swapped(own, "zl", j) for j in (3, 2))
    x2, x1, x3 = (swapped(own, "x", i) for i in (2, 1, 3))
    blocks = [jnp.stack([own, x1, x2, x3, z2, z3])]
    spots = [[(0, 0), (1, 0), (2, 0), (3, 0), (0, 2), (0, 3)]]
    blocks.append(swapped(blocks[0][:4], "zl", 1))
    spots.append([(i, 1) for i in range(4)])
    for i in (2, 1, 3):
        blocks.append(swapped(jnp.stack([z2, z3]), "x", i))
        spots.append([(i, 2), (i, 3)])
    return blocks, spots


def on_device(signal, kx_index, kz_index):
    width = signal.shape[-1]
    y, zh, core = (lax.axis_index(name) for name in SPEC)
    at = lax.axis_index(SPEC) * width
    place = jnp.stack([at, y, zh, core, lax.axis_index("x"), lax.axis_index("zl")]).astype(jnp.int32)
    mine, other = dft(place, kx_index, kz_index, signal)
    summed = mine + shifted(other, "core", 1)
    came = [shifted(summed[i], "y", i) for i in (2, 1, 3)]
    halves = summed[0] + came[0] + came[1] + came[2]
    own = turn(halves[0], shifted(halves[1], "zh", 1))
    return gram(place, own, *gathered(own))


def solution(mesh):
    fine = Mesh(mesh.devices.reshape(4, 4, 4, 2, 2), FINE)
    return jax.shard_map(
        on_device,
        mesh=fine,
        in_specs=(P(None, None, WALL, None, SPEC), P(), P()),
        out_specs=P(None, SPEC, WALL, None),
        check_vma=False,
    )
```

```python
import functools
import math

import jax
import jax.numpy as jnp
from jax import lax
from jax.experimental import pallas as pl
from jax.experimental.pallas import tpu as pltpu
from jax.sharding import Mesh
from jax.sharding import PartitionSpec as P

NXW = 10240
QUARTER = NXW // 4
SIN = (1.0, -1.0 / 6, 1.0 / 120, -1.0 / 5040, 1.0 / 362880)
COS = (1.0, -0.5, 1.0 / 24, -1.0 / 720, 1.0 / 40320)
FINE = ("x", "zl", "y", "zh", "core")
WALL, SPEC = FINE[:2], FINE[2:]
VMEM = pl.BlockSpec(memory_space=pltpu.VMEM)
SMEM = pl.BlockSpec(memory_space=pltpu.SMEM)
HBM = pl.BlockSpec(memory_space=pl.ANY)
FAR = pl.BlockSpec(memory_space=pltpu.HBM)
PARAMS = pltpu.CompilerParams(vmem_limit_bytes=48 * 2**20)


def horner(coefficients, square):
    total = jnp.full_like(square, coefficients[-1])
    for value in coefficients[-2::-1]:
        total = total * square + value
    return total


def basis_columns(kx_row, positions):
    product = positions * kx_row
    quarter = jnp.floor(product.astype(jnp.float32) * (1.0 / QUARTER) + 0.5).astype(jnp.int32)
    angle = (product - quarter * QUARTER).astype(jnp.float32) * (2.0 * math.pi / NXW)
    square = angle * angle
    sine = horner(SIN, square) * angle
    cosine = horner(COS, square)
    swap = (quarter & 1) == 1
    factor = float(NXW) ** -0.5
    first = jnp.where(swap, sine, cosine) * factor
    second = jnp.where(swap, cosine, sine) * factor
    first = jnp.where(((quarter + 1) & 2) == 2, -first, first)
    second = jnp.where((quarter & 2) == 2, -second, second)
    return first.astype(jnp.bfloat16), second.astype(jnp.bfloat16)


CHUNKS = (2, 2, 2, 2)


def dft_kernel(place, kx_hbm, kz_hbm, signal, own_mine, own_other, far_mine, far_other, held, basis, kx_ref, kz_ref, sems):
    modes, parts, quads, groups, snaps, width = signal.shape
    pairs = kx_ref.shape[1]
    index = [
        pltpu.make_async_copy(kx_hbm, kx_ref, sems.at[len(CHUNKS)]),
        pltpu.make_async_copy(kz_hbm, kz_ref, sems.at[len(CHUNKS) + 1]),
    ]
    for copy in index:
        copy.start()
    copies, first = [], 0
    for t, size in enumerate(CHUNKS):
        part = pl.ds(first, size)
        copies.append(pltpu.make_async_copy(signal.at[:, :, :, part], held.at[:, :, :, part], sems.at[t]))
        copies[t].start()
        first += size
    for copy in index:
        copy.wait()
    rows = lax.broadcasted_iota(jnp.int32, (width, pairs), 0) + place[0]
    cosine, sine = basis_columns(kx_ref[...], rows)
    basis[:width, :pairs] = cosine
    basis[:width, pairs:] = -sine
    basis[width:, :pairs] = sine
    basis[width:, pairs:] = cosine
    kz = jnp.concatenate([kz_ref[...], kz_ref[...]], axis=1)
    y, zh, core = place[1], place[2], place[3]
    first = 0
    for t, size in enumerate(CHUNKS):
        copies[t].wait()
        total = None
        for j in range(modes):
            lines = []
            for g in range(first, first + size):
                halves = [held[j, c, :, g].reshape(quads * snaps, width) for c in range(parts)]
                lines.append(jnp.concatenate(halves, axis=1))
            lines = jnp.concatenate(lines, axis=0)
            product = jnp.dot(lines, basis[...], preferred_element_type=jnp.float32)
            total = product if total is None else jnp.where(kz == j, product, total)
        for i in range(size):
            turned = total[i * 128 : (i + 1) * 128].T
            for yy in range(4):
                slot = (yy + 4 - y) & 3
                for c in range(parts):
                    tiles = []
                    for zz in range(2):
                        at = c * pairs + (yy * 4 + zz * 2) * 8
                        low, high = turned[at : at + 8], turned[at + 8 : at + 16]
                        tiles.append((jnp.where(core == 0, low, high), jnp.where(core == 0, high, low)))
                    for n, (own, far) in enumerate(((own_mine, far_mine), (own_other, far_other))):
                        own[slot, c, first + i] = jnp.where(zh == 0, tiles[0][n], tiles[1][n])
                        far[slot, c, first + i] = jnp.where(zh == 0, tiles[1][n], tiles[0][n])
        first += size


def dft(place, kx_index, kz_index, signal):
    modes, parts, planes, snaps, width = signal.shape
    pairs = kx_index.shape[0]
    view = signal.reshape(modes, parts, 4, planes // 4, snaps, width)
    block = jax.ShapeDtypeStruct((4, parts, planes // 4, 8, 128), jnp.float32)
    return pl.pallas_call(
        dft_kernel,
        out_shape=(block,) * 4,
        in_specs=[SMEM, FAR, FAR, HBM],
        out_specs=(VMEM,) * 4,
        scratch_shapes=[
            pltpu.VMEM(view.shape, signal.dtype),
            pltpu.VMEM((parts * width, 2 * pairs), jnp.bfloat16),
            pltpu.VMEM((1, pairs), jnp.int32),
            pltpu.VMEM((1, pairs), jnp.int32),
            pltpu.SemaphoreType.DMA((len(CHUNKS) + 2,)),
        ],
        compiler_params=PARAMS,
        name="dft",
    )(
        place,
        pltpu.with_memory_space_constraint(kx_index.reshape(1, pairs), pltpu.HBM),
        pltpu.with_memory_space_constraint(kz_index.reshape(1, pairs), pltpu.HBM),
        view,
    )


def turn_kernel(own_ref, came_ref, out_ref, total):
    total[...] = own_ref[...].reshape(total.shape) + came_ref[...].reshape(total.shape)
    lane = lax.broadcasted_iota(jnp.int32, (8, 128), 1) // 32
    for kk in range(4):
        tiles = []
        for k2 in range(2):
            for c in range(2):
                tiles.append(total[c, pl.ds(2 * kk + k2, 8, stride=8), :])
        for q in range(4):
            row = None
            for j, tile in enumerate(tiles):
                shift = ((j - q) * 32) % 128
                moved = tile if shift == 0 else pltpu.roll(tile, shift, 1)
                row = moved if row is None else jnp.where(lane == j, moved, row)
            out_ref[kk, q * 8 : (q + 1) * 8, :] = row


def turn(own, came):
    return pl.pallas_call(
        turn_kernel,
        out_shape=jax.ShapeDtypeStruct((4, 32, 128), jnp.float32),
        in_specs=[VMEM, VMEM],
        out_specs=VMEM,
        scratch_shapes=[pltpu.VMEM((2, 64, 128), jnp.float32)],
        compiler_params=PARAMS,
        name="turn",
    )(own, came)


def against(left, right):
    return lax.dot_general(left, right, (((1,), (1,)), ((), ())), preferred_element_type=jnp.float32)


def gram_kernel(spots, place, own_ref, *refs):
    blocks, (out_hbm, right, out, sems) = refs[:-4], refs[-4:]
    x, zl = place[4], place[5]
    lane = lax.broadcasted_iota(jnp.int32, (32, 128), 1) // 32
    copies = []
    for kk in range(4):
        for block, group in zip(blocks, spots):
            for n, (i, j) in enumerate(group):
                at = pl.multiple_of(((x ^ i) * 4 + (zl ^ j)) * 32, 32)
                right[kk, pl.ds(at, 32), :] = block[n, kk].astype(jnp.bfloat16)
        own = own_ref[kk] * (1.0 / 32)
        turned = jnp.where(lane % 2 == 0, pltpu.roll(own, 96, 1), -pltpu.roll(own, 32, 1))
        left = []
        for k2 in range(2):
            keep = lane // 2 == k2
            left.append(jnp.where(keep, own, 0.0))
            left.append(jnp.where(keep, turned, 0.0))
        whole = jnp.concatenate(left, axis=0)
        high = whole.astype(jnp.bfloat16)
        low = (whole - high.astype(jnp.float32)).astype(jnp.bfloat16)
        product = against(jnp.concatenate([high, low], axis=1), jnp.concatenate([right[kk], right[kk]], axis=1))
        for k2 in range(2):
            for c in range(2):
                base = (k2 * 2 + c) * 32
                out[c, 2 * kk + k2] = product[base : base + 32]
        part = pl.ds(2 * kk, 2)
        copies.append(pltpu.make_async_copy(out.at[:, part], out_hbm.at[:, part], sems.at[kk]))
        copies[kk].start()
    for copy in copies:
        copy.wait()


def gram(place, own, blocks, spots):
    shape = (2, 8, 32, 512)
    return pl.pallas_call(
        functools.partial(gram_kernel, spots),
        out_shape=jax.ShapeDtypeStruct(shape, jnp.float32),
        in_specs=[SMEM, VMEM] + [VMEM] * len(blocks),
        out_specs=HBM,
        scratch_shapes=[
            pltpu.VMEM((4, 512, 128), jnp.bfloat16),
            pltpu.VMEM(shape, jnp.float32),
            pltpu.SemaphoreType.DMA((4,)),
        ],
        compiler_params=PARAMS,
        name="gram",
    )(place, own, *blocks)


def shifted(array, axis, by):
    size = lax.axis_size(axis)
    return lax.ppermute(array, axis, [(s, (s + by) % size) for s in range(size)])


def swapped(array, axis, by):
    return lax.ppermute(array, axis, [(s, s ^ by) for s in range(lax.axis_size(axis))])


def gathered(own):
    z3, z2 = (swapped(own, "zl", j) for j in (3, 2))
    x1, x2, x3 = (swapped(own, "x", i) for i in (1, 2, 3))
    blocks = [jnp.stack([own, x1, x2, x3, z2, z3])]
    spots = [[(0, 0), (1, 0), (2, 0), (3, 0), (0, 2), (0, 3)]]
    blocks.append(swapped(blocks[0][:4], "zl", 1))
    spots.append([(i, 1) for i in range(4)])
    for i in (1, 2, 3):
        blocks.append(swapped(jnp.stack([z2, z3]), "x", i))
        spots.append([(i, 2), (i, 3)])
    return blocks, spots


def summed_over_y(mine, other):
    summed = mine + swapped(other, "core", 1)
    came = [shifted(summed[i], "y", i) for i in (1, 2, 3)]
    return summed[0] + came[0] + came[1] + came[2]


def on_device(signal, kx_index, kz_index):
    width = signal.shape[-1]
    y, zh, core = (lax.axis_index(name) for name in SPEC)
    at = lax.axis_index(SPEC) * width
    place = jnp.stack([at, y, zh, core, lax.axis_index("x"), lax.axis_index("zl")]).astype(jnp.int32)
    own_mine, own_other, far_mine, far_other = dft(place, kx_index, kz_index, signal)
    far = summed_over_y(far_mine, far_other)
    came = swapped(far, "zh", 1)
    own = turn(summed_over_y(own_mine, own_other), came)
    return gram(place, own, *gathered(own))


def solution(mesh):
    fine = Mesh(mesh.devices.reshape(4, 4, 4, 2, 2), FINE)
    return jax.shard_map(
        on_device,
        mesh=fine,
        in_specs=(P(None, None, WALL, None, SPEC), P(), P()),
        out_specs=P(None, SPEC, WALL, None),
        check_vma=False,
    )
```

```python
import functools
import math

import jax
import jax.numpy as jnp
from jax import lax
from jax.experimental import pallas as pl
from jax.experimental.pallas import tpu as pltpu
from jax.sharding import Mesh
from jax.sharding import PartitionSpec as P

NXW = 10240
QUARTER = NXW // 4
SIN = (1.0, -1.0 / 6, 1.0 / 120, -1.0 / 5040, 1.0 / 362880)
COS = (1.0, -0.5, 1.0 / 24, -1.0 / 720, 1.0 / 40320)
FINE = ("x", "zl", "y", "zh", "core")
WALL, SPEC = FINE[:2], FINE[2:]
VMEM = pl.BlockSpec(memory_space=pltpu.VMEM)
SMEM = pl.BlockSpec(memory_space=pltpu.SMEM)
HBM = pl.BlockSpec(memory_space=pl.ANY)
FAR = pl.BlockSpec(memory_space=pltpu.HBM)
PARAMS = pltpu.CompilerParams(vmem_limit_bytes=48 * 2**20)


def horner(coefficients, square):
    total = jnp.full_like(square, coefficients[-1])
    for value in coefficients[-2::-1]:
        total = total * square + value
    return total


def basis_columns(kx_row, positions):
    product = positions * kx_row
    quarter = jnp.floor(product.astype(jnp.float32) * (1.0 / QUARTER) + 0.5).astype(jnp.int32)
    angle = (product - quarter * QUARTER).astype(jnp.float32) * (2.0 * math.pi / NXW)
    square = angle * angle
    sine = horner(SIN, square) * angle
    cosine = horner(COS, square)
    swap = (quarter & 1) == 1
    factor = float(NXW) ** -0.5
    first = jnp.where(swap, sine, cosine) * factor
    second = jnp.where(swap, cosine, sine) * factor
    first = jnp.where(((quarter + 1) & 2) == 2, -first, first)
    second = jnp.where((quarter & 2) == 2, -second, second)
    return first.astype(jnp.bfloat16), second.astype(jnp.bfloat16)


CHUNKS = (2, 2, 2, 2)


def dft_kernel(place, kx_hbm, kz_hbm, signal, own_mine, own_other, far_mine, far_other, held, basis, kx_ref, kz_ref, sems):
    modes, parts, quads, groups, snaps, width = signal.shape
    pairs = kx_ref.shape[1]
    index = [
        pltpu.make_async_copy(kx_hbm, kx_ref, sems.at[len(CHUNKS)]),
        pltpu.make_async_copy(kz_hbm, kz_ref, sems.at[len(CHUNKS) + 1]),
    ]
    for copy in index:
        copy.start()
    copies, first = [], 0
    for t, size in enumerate(CHUNKS):
        part = pl.ds(first, size)
        copies.append(pltpu.make_async_copy(signal.at[:, :, :, part], held.at[:, :, :, part], sems.at[t]))
        copies[t].start()
        first += size
    for copy in index:
        copy.wait()
    rows = lax.broadcasted_iota(jnp.int32, (width, pairs), 0) + place[0]
    cosine, sine = basis_columns(kx_ref[...], rows)
    basis[:width, :pairs] = cosine
    basis[:width, pairs:] = -sine
    basis[width:, :pairs] = sine
    basis[width:, pairs:] = cosine
    kz = jnp.concatenate([kz_ref[...], kz_ref[...]], axis=1)
    y, zh, core = place[1], place[2], place[3]
    first = 0
    for t, size in enumerate(CHUNKS):
        copies[t].wait()
        total = None
        for j in range(modes):
            lines = []
            for g in range(first, first + size):
                halves = [held[j, c, :, g].reshape(quads * snaps, width) for c in range(parts)]
                lines.append(jnp.concatenate(halves, axis=1))
            lines = jnp.concatenate(lines, axis=0)
            product = jnp.dot(lines, basis[...], preferred_element_type=jnp.float32)
            total = product if total is None else jnp.where(kz == j, product, total)
        for i in range(size):
            turned = total[i * 128 : (i + 1) * 128].T
            for yy in range(4):
                slot = (yy + 4 - y) & 3
                for c in range(parts):
                    tiles = []
                    for zz in range(2):
                        at = c * pairs + (yy * 4 + zz * 2) * 8
                        low, high = turned[at : at + 8], turned[at + 8 : at + 16]
                        tiles.append((jnp.where(core == 0, low, high), jnp.where(core == 0, high, low)))
                    for n, (own, far) in enumerate(((own_mine, far_mine), (own_other, far_other))):
                        own[slot, c, first + i] = jnp.where(zh == 0, tiles[0][n], tiles[1][n])
                        far[slot, c, first + i] = jnp.where(zh == 0, tiles[1][n], tiles[0][n])
        first += size


def dft(place, kx_index, kz_index, signal):
    modes, parts, planes, snaps, width = signal.shape
    pairs = kx_index.shape[0]
    view = signal.reshape(modes, parts, 4, planes // 4, snaps, width)
    block = jax.ShapeDtypeStruct((4, parts, planes // 4, 8, 128), jnp.float32)
    return pl.pallas_call(
        dft_kernel,
        out_shape=(block,) * 4,
        in_specs=[SMEM, FAR, FAR, HBM],
        out_specs=(VMEM,) * 4,
        scratch_shapes=[
            pltpu.VMEM(view.shape, signal.dtype),
            pltpu.VMEM((parts * width, 2 * pairs), jnp.bfloat16),
            pltpu.VMEM((1, pairs), jnp.int32),
            pltpu.VMEM((1, pairs), jnp.int32),
            pltpu.SemaphoreType.DMA((len(CHUNKS) + 2,)),
        ],
        compiler_params=PARAMS,
        name="dft",
    )(
        place,
        pltpu.with_memory_space_constraint(kx_index.reshape(1, pairs), pltpu.HBM),
        pltpu.with_memory_space_constraint(kz_index.reshape(1, pairs), pltpu.HBM),
        view,
    )


def turn_kernel(own_ref, came_ref, out_ref, total):
    total[...] = own_ref[...].reshape(total.shape) + came_ref[...].reshape(total.shape)
    lane = lax.broadcasted_iota(jnp.int32, (8, 128), 1) // 32
    for kk in range(4):
        tiles = []
        for k2 in range(2):
            for c in range(2):
                tiles.append(total[c, pl.ds(2 * kk + k2, 8, stride=8), :])
        for q in range(4):
            row = None
            for j, tile in enumerate(tiles):
                shift = ((j - q) * 32) % 128
                moved = tile if shift == 0 else pltpu.roll(tile, shift, 1)
                row = moved if row is None else jnp.where(lane == j, moved, row)
            out_ref[kk, q * 8 : (q + 1) * 8, :] = row


def turn(own, came):
    return pl.pallas_call(
        turn_kernel,
        out_shape=jax.ShapeDtypeStruct((4, 32, 128), jnp.float32),
        in_specs=[VMEM, VMEM],
        out_specs=VMEM,
        scratch_shapes=[pltpu.VMEM((2, 64, 128), jnp.float32)],
        compiler_params=PARAMS,
        name="turn",
    )(own, came)


def against(left, right):
    return lax.dot_general(left, right, (((1,), (1,)), ((), ())), preferred_element_type=jnp.float32)


def gram_kernel(spots, place, own_ref, *refs):
    blocks, (out_hbm, right, out, sems) = refs[:-4], refs[-4:]
    x, zl = place[4], place[5]
    lane = lax.broadcasted_iota(jnp.int32, (32, 128), 1) // 32
    copies = []
    for kk in range(4):
        for block, group in zip(blocks, spots):
            for n, (i, j) in enumerate(group):
                at = pl.multiple_of(((x ^ i) * 4 + (zl ^ j)) * 32, 32)
                right[kk, pl.ds(at, 32), :] = block[n, kk].astype(jnp.bfloat16)
        own = own_ref[kk] * (1.0 / 32)
        turned = jnp.where(lane % 2 == 0, pltpu.roll(own, 96, 1), -pltpu.roll(own, 32, 1))
        left = []
        for k2 in range(2):
            keep = lane // 2 == k2
            left.append(jnp.where(keep, own, 0.0))
            left.append(jnp.where(keep, turned, 0.0))
        whole = jnp.concatenate(left, axis=0)
        high = whole.astype(jnp.bfloat16)
        low = (whole - high.astype(jnp.float32)).astype(jnp.bfloat16)
        product = against(jnp.concatenate([high, low], axis=1), jnp.concatenate([right[kk], right[kk]], axis=1))
        for k2 in range(2):
            for c in range(2):
                base = (k2 * 2 + c) * 32
                out[c, 2 * kk + k2] = product[base : base + 32]
        part = pl.ds(2 * kk, 2)
        copies.append(pltpu.make_async_copy(out.at[:, part], out_hbm.at[:, part], sems.at[kk]))
        copies[kk].start()
    for copy in copies:
        copy.wait()


def gram(place, own, blocks, spots):
    shape = (2, 8, 32, 512)
    return pl.pallas_call(
        functools.partial(gram_kernel, spots),
        out_shape=jax.ShapeDtypeStruct(shape, jnp.float32),
        in_specs=[SMEM, VMEM] + [VMEM] * len(blocks),
        out_specs=HBM,
        scratch_shapes=[
            pltpu.VMEM((4, 512, 128), jnp.bfloat16),
            pltpu.VMEM(shape, jnp.float32),
            pltpu.SemaphoreType.DMA((4,)),
        ],
        compiler_params=PARAMS,
        name="gram",
    )(place, own, *blocks)


def shifted(array, axis, by):
    size = lax.axis_size(axis)
    return lax.ppermute(array, axis, [(s, (s + by) % size) for s in range(size)])


def swapped(array, axis, by):
    return lax.ppermute(array, axis, [(s, s ^ by) for s in range(lax.axis_size(axis))])


def gathered(own):
    z3, z2 = (swapped(own, "zl", j) for j in (3, 2))
    x1, x2, x3 = (swapped(own, "x", i) for i in (1, 2, 3))
    blocks = [jnp.stack([own, x1, x2, x3, z2, z3])]
    spots = [[(0, 0), (1, 0), (2, 0), (3, 0), (0, 2), (0, 3)]]
    blocks.append(swapped(blocks[0][:4], "zl", 1))
    spots.append([(i, 1) for i in range(4)])
    for i in (1, 2, 3):
        blocks.append(swapped(jnp.stack([z2, z3]), "x", i))
        spots.append([(i, 2), (i, 3)])
    return blocks, spots


def summed_over_y(mine, other):
    summed = mine + swapped(other, "core", 1)
    came = [shifted(summed[i], "y", i) for i in (1, 3, 2)]
    return summed[0] + came[0] + came[1] + came[2]


def on_device(signal, kx_index, kz_index):
    width = signal.shape[-1]
    y, zh, core = (lax.axis_index(name) for name in SPEC)
    at = lax.axis_index(SPEC) * width
    place = jnp.stack([at, y, zh, core, lax.axis_index("x"), lax.axis_index("zl")]).astype(jnp.int32)
    own_mine, own_other, far_mine, far_other = dft(place, kx_index, kz_index, signal)
    far = summed_over_y(far_mine, far_other)
    came = swapped(far, "zh", 1)
    own = turn(summed_over_y(own_mine, own_other), came)
    return gram(place, own, *gathered(own))


def solution(mesh):
    fine = Mesh(mesh.devices.reshape(4, 4, 4, 2, 2), FINE)
    return jax.shard_map(
        on_device,
        mesh=fine,
        in_specs=(P(None, None, WALL, None, SPEC), P(), P()),
        out_specs=P(None, SPEC, WALL, None),
        check_vma=False,
    )
```

```python
import functools
import math

import jax
import jax.numpy as jnp
from jax import lax
from jax.experimental import pallas as pl
from jax.experimental.pallas import tpu as pltpu
from jax.sharding import Mesh
from jax.sharding import PartitionSpec as P

NXW = 10240
QUARTER = NXW // 4
SIN = (1.0, -1.0 / 6, 1.0 / 120, -1.0 / 5040, 1.0 / 362880)
COS = (1.0, -0.5, 1.0 / 24, -1.0 / 720, 1.0 / 40320)
FINE = ("x", "zl", "y", "zh", "core")
WALL, SPEC = FINE[:2], FINE[2:]
VMEM = pl.BlockSpec(memory_space=pltpu.VMEM)
SMEM = pl.BlockSpec(memory_space=pltpu.SMEM)
HBM = pl.BlockSpec(memory_space=pl.ANY)
FAR = pl.BlockSpec(memory_space=pltpu.HBM)
PARAMS = pltpu.CompilerParams(vmem_limit_bytes=48 * 2**20)


def horner(coefficients, square):
    total = jnp.full_like(square, coefficients[-1])
    for value in coefficients[-2::-1]:
        total = total * square + value
    return total


def basis_columns(kx_row, positions):
    product = positions * kx_row
    quarter = jnp.floor(product.astype(jnp.float32) * (1.0 / QUARTER) + 0.5).astype(jnp.int32)
    angle = (product - quarter * QUARTER).astype(jnp.float32) * (2.0 * math.pi / NXW)
    square = angle * angle
    sine = horner(SIN, square) * angle
    cosine = horner(COS, square)
    swap = (quarter & 1) == 1
    factor = float(NXW) ** -0.5
    first = jnp.where(swap, sine, cosine) * factor
    second = jnp.where(swap, cosine, sine) * factor
    first = jnp.where(((quarter + 1) & 2) == 2, -first, first)
    second = jnp.where((quarter & 2) == 2, -second, second)
    return first.astype(jnp.bfloat16), second.astype(jnp.bfloat16)


CHUNKS = (2, 2, 2, 2)


def dft_kernel(place, kx_hbm, kz_hbm, signal, own_mine, own_other, far_mine, far_other, held, basis, kx_ref, kz_ref, sems):
    modes, parts, quads, groups, snaps, width = signal.shape
    pairs = kx_ref.shape[1]
    index = [
        pltpu.make_async_copy(kx_hbm, kx_ref, sems.at[len(CHUNKS)]),
        pltpu.make_async_copy(kz_hbm, kz_ref, sems.at[len(CHUNKS) + 1]),
    ]
    for copy in index:
        copy.start()
    copies, first = [], 0
    for t, size in enumerate(CHUNKS):
        part = pl.ds(first, size)
        copies.append(pltpu.make_async_copy(signal.at[:, :, :, part], held.at[:, :, :, part], sems.at[t]))
        copies[t].start()
        first += size
    for copy in index:
        copy.wait()
    rows = lax.broadcasted_iota(jnp.int32, (width, pairs), 0) + place[0]
    cosine, sine = basis_columns(kx_ref[...], rows)
    basis[:width, :pairs] = cosine
    basis[:width, pairs:] = -sine
    basis[width:, :pairs] = sine
    basis[width:, pairs:] = cosine
    kz = jnp.concatenate([kz_ref[...], kz_ref[...]], axis=1)
    y, zh, core = place[1], place[2], place[3]
    first = 0
    for t, size in enumerate(CHUNKS):
        copies[t].wait()
        total = None
        for j in range(modes):
            lines = []
            for g in range(first, first + size):
                halves = [held[j, c, :, g].reshape(quads * snaps, width) for c in range(parts)]
                lines.append(jnp.concatenate(halves, axis=1))
            lines = jnp.concatenate(lines, axis=0)
            product = jnp.dot(lines, basis[...], preferred_element_type=jnp.float32)
            total = product if total is None else jnp.where(kz == j, product, total)
        for i in range(size):
            turned = total[i * 128 : (i + 1) * 128].T
            for yy in range(4):
                slot = (yy + 4 - y) & 3
                for c in range(parts):
                    tiles = []
                    for zz in range(2):
                        at = c * pairs + (yy * 4 + zz * 2) * 8
                        low, high = turned[at : at + 8], turned[at + 8 : at + 16]
                        tiles.append((jnp.where(core == 0, low, high), jnp.where(core == 0, high, low)))
                    for n, (own, far) in enumerate(((own_mine, far_mine), (own_other, far_other))):
                        own[slot, c, first + i] = jnp.where(zh == 0, tiles[0][n], tiles[1][n])
                        far[slot, c, first + i] = jnp.where(zh == 0, tiles[1][n], tiles[0][n])
        first += size


def dft(place, kx_index, kz_index, signal):
    modes, parts, planes, snaps, width = signal.shape
    pairs = kx_index.shape[0]
    view = signal.reshape(modes, parts, 4, planes // 4, snaps, width)
    block = jax.ShapeDtypeStruct((4, parts, planes // 4, 8, 128), jnp.float32)
    return pl.pallas_call(
        dft_kernel,
        out_shape=(block,) * 4,
        in_specs=[SMEM, FAR, FAR, HBM],
        out_specs=(VMEM,) * 4,
        scratch_shapes=[
            pltpu.VMEM(view.shape, signal.dtype),
            pltpu.VMEM((parts * width, 2 * pairs), jnp.bfloat16),
            pltpu.VMEM((1, pairs), jnp.int32),
            pltpu.VMEM((1, pairs), jnp.int32),
            pltpu.SemaphoreType.DMA((len(CHUNKS) + 2,)),
        ],
        compiler_params=PARAMS,
        name="dft",
    )(
        place,
        pltpu.with_memory_space_constraint(kx_index.reshape(1, pairs), pltpu.HBM),
        pltpu.with_memory_space_constraint(kz_index.reshape(1, pairs), pltpu.HBM),
        view,
    )


def turn_kernel(own_ref, came_ref, out_ref, total):
    total[...] = own_ref[...].reshape(total.shape) + came_ref[...].reshape(total.shape)
    lane = lax.broadcasted_iota(jnp.int32, (8, 128), 1) // 32
    for kk in range(4):
        tiles = []
        for k2 in range(2):
            for c in range(2):
                tiles.append(total[c, pl.ds(2 * kk + k2, 8, stride=8), :])
        for q in range(4):
            row = None
            for j, tile in enumerate(tiles):
                shift = ((j - q) * 32) % 128
                moved = tile if shift == 0 else pltpu.roll(tile, shift, 1)
                row = moved if row is None else jnp.where(lane == j, moved, row)
            out_ref[kk, q * 8 : (q + 1) * 8, :] = row


def turn(own, came):
    return pl.pallas_call(
        turn_kernel,
        out_shape=jax.ShapeDtypeStruct((4, 32, 128), jnp.float32),
        in_specs=[VMEM, VMEM],
        out_specs=VMEM,
        scratch_shapes=[pltpu.VMEM((2, 64, 128), jnp.float32)],
        compiler_params=PARAMS,
        name="turn",
    )(own, came)


def against(left, right):
    return lax.dot_general(left, right, (((1,), (1,)), ((), ())), preferred_element_type=jnp.float32)


def place_blocks(place, blocks, spots, kk, right):
    x, zl = place[4], place[5]
    for block, group in zip(blocks, spots):
        for n, (i, j) in enumerate(group):
            at = pl.multiple_of(((x ^ i) * 4 + (zl ^ j)) * 32, 32)
            right[kk, pl.ds(at, 32), :] = block[n, kk].astype(jnp.bfloat16)


def prepare_kernel(spots, place, own_ref, block, left_ref, right):
    lane = lax.broadcasted_iota(jnp.int32, (32, 128), 1) // 32
    for kk in range(4):
        place_blocks(place, [block], spots, kk, right)
        own = own_ref[kk] * (1.0 / 32)
        turned = jnp.where(lane % 2 == 0, pltpu.roll(own, 96, 1), -pltpu.roll(own, 32, 1))
        left = []
        for k2 in range(2):
            keep = lane // 2 == k2
            left.append(jnp.where(keep, own, 0.0))
            left.append(jnp.where(keep, turned, 0.0))
        whole = jnp.concatenate(left, axis=0)
        high = whole.astype(jnp.bfloat16)
        low = (whole - high.astype(jnp.float32)).astype(jnp.bfloat16)
        left_ref[kk] = jnp.concatenate([high, low], axis=1)


def gram_kernel(spots, place, left_ref, right_in, *refs):
    blocks, (out_hbm, right, out, sems) = refs[:-4], refs[-4:]
    copies = []
    for kk in range(4):
        place_blocks(place, blocks, spots, kk, right)
        product = against(left_ref[kk], jnp.concatenate([right[kk], right[kk]], axis=1))
        for k2 in range(2):
            for c in range(2):
                base = (k2 * 2 + c) * 32
                out[c, 2 * kk + k2] = product[base : base + 32]
        part = pl.ds(2 * kk, 2)
        copies.append(pltpu.make_async_copy(out.at[:, part], out_hbm.at[:, part], sems.at[kk]))
        copies[kk].start()
    for copy in copies:
        copy.wait()


def gram(place, own, blocks, spots):
    shape = (2, 8, 32, 512)
    right_shape = jax.ShapeDtypeStruct((4, 512, 128), jnp.bfloat16)
    left, right = pl.pallas_call(
        functools.partial(prepare_kernel, spots[:1]),
        out_shape=(jax.ShapeDtypeStruct((4, 128, 256), jnp.bfloat16), right_shape),
        in_specs=[SMEM, VMEM, VMEM],
        out_specs=(VMEM, VMEM),
        compiler_params=PARAMS,
        name="prepare",
    )(place, own, blocks[0])
    return pl.pallas_call(
        functools.partial(gram_kernel, spots[1:]),
        out_shape=(jax.ShapeDtypeStruct(shape, jnp.float32), right_shape),
        in_specs=[SMEM] + [VMEM] * (1 + len(blocks)),
        out_specs=(HBM, VMEM),
        input_output_aliases={2: 1},
        scratch_shapes=[pltpu.VMEM(shape, jnp.float32), pltpu.SemaphoreType.DMA((4,))],
        compiler_params=PARAMS,
        name="gram",
    )(place, left, right, *blocks[1:])[0]


def shifted(array, axis, by):
    size = lax.axis_size(axis)
    return lax.ppermute(array, axis, [(s, (s + by) % size) for s in range(size)])


def swapped(array, axis, by):
    return lax.ppermute(array, axis, [(s, s ^ by) for s in range(lax.axis_size(axis))])


def gathered(own):
    z3, z2 = (swapped(own, "zl", j) for j in (3, 2))
    x1, x2, x3 = (swapped(own, "x", i) for i in (1, 2, 3))
    blocks = [jnp.stack([own, x1, x2, x3, z2, z3])]
    spots = [[(0, 0), (1, 0), (2, 0), (3, 0), (0, 2), (0, 3)]]
    blocks.append(swapped(blocks[0][:4], "zl", 1))
    spots.append([(i, 1) for i in range(4)])
    for i in (1, 2, 3):
        blocks.append(swapped(jnp.stack([z2, z3]), "x", i))
        spots.append([(i, 2), (i, 3)])
    return blocks, spots


def summed_over_y(mine, other):
    summed = mine + swapped(other, "core", 1)
    came = [shifted(summed[i], "y", i) for i in (1, 3, 2)]
    return summed[0] + came[0] + came[1] + came[2]


def on_device(signal, kx_index, kz_index):
    width = signal.shape[-1]
    y, zh, core = (lax.axis_index(name) for name in SPEC)
    at = lax.axis_index(SPEC) * width
    place = jnp.stack([at, y, zh, core, lax.axis_index("x"), lax.axis_index("zl")]).astype(jnp.int32)
    own_mine, own_other, far_mine, far_other = dft(place, kx_index, kz_index, signal)
    far = summed_over_y(far_mine, far_other)
    came = swapped(far, "zh", 1)
    own = turn(summed_over_y(own_mine, own_other), came)
    return gram(place, own, *gathered(own))


def solution(mesh):
    fine = Mesh(mesh.devices.reshape(4, 4, 4, 2, 2), FINE)
    return jax.shard_map(
        on_device,
        mesh=fine,
        in_specs=(P(None, None, WALL, None, SPEC), P(), P()),
        out_specs=P(None, SPEC, WALL, None),
        check_vma=False,
    )
```
